32 devices in a mesh: rep: 4 (over y, core), fsdp: 8 (over z, x).
Axes of the slice: x: 2, y: 2, z: 4, core: 2. Of those that a mesh axis runs over, the one named last changes fastest.
Arguments:
- activations: bfloat16 [4, 3072, 4096], P('rep', 'fsdp'), may hold values from -6 to 6
- key_cotangent: bfloat16 [4, 3072, 512], P('rep', 'fsdp'), may hold values from -12 to 12
- doc_ids: int32 [4, 3072], P('rep', 'fsdp'), may hold values from 0 to 7, as said below
- replica_params: float32 [4, 4096, 512], P('rep', 'fsdp'), may hold values from -14 to 14
- first_moment: float32 [4, 4096, 512], P('rep', 'fsdp'), may hold values from -6 to 6
- second_moment: float32 [4, 4096, 512], P('rep', 'fsdp'), may hold values from 1 to 16
- anchor: float32 [4096, 512], P(('fsdp', 'rep')), may hold values from -8 to 8
- momentum: float32 [4096, 512], P(('fsdp', 'rep')), may hold values from -3 to 3
Outputs:
- new_first: float32 [4, 4096, 512], P('rep', 'fsdp')
- new_second: float32 [4, 4096, 512], P('rep', 'fsdp')
- new_momentum: float32 [4096, 512], P(('fsdp', 'rep'))
- new_params: float32 [4096, 512], P('fsdp')
The draws below stay inside these ranges and needn't reach their ends.
Inputs may be any that keep to these rules, and one draw needn't show every extreme that they name: `doc_ids`: within each group the numbers never fall along the tokens; every block of 384 consecutive tokens (from token 0) holds the first token of exactly one document; every document holds 1 to 767 tokens and one holds exactly 767.
All inputs are finite; a program needn't handle non-finite values.
Results may differ from the reference program's by a relative error of at most 0.0035.
Values may be sent and summed in bfloat16 or wider, within the bound.
No kernel may reach another device: no remote copies, remote signals or barrier semaphores. Data moves between devices by JAX's collectives and lax.ppermute only.
A program may use at most 64 MiB of HBM per device.

```python
import math
import jax
import jax.numpy as jnp
from jax import lax

DW = 4096
KV_HEADS = 4
HEAD = 128
TOK_DEV = 384
KVW = 512
REPS = 4
TOKENS = 3072
N_REP = 4
N_FSDP = 8


def common_anchor(key):
    anchor_key = jax.random.fold_in(key, 7)
    return jax.random.normal(anchor_key, (DW, KV_HEADS * HEAD), jnp.float32)


def draw_anchor(key, part):
    return common_anchor(key)


def draw_replica_params(key, part):
    drift_key = jax.random.fold_in(key, 19)
    drift = jax.random.normal(drift_key, (REPS, DW, KV_HEADS * HEAD), jnp.float32)
    return common_anchor(key)[None, :, :] + drift


def draw_doc_ids(key, part):
    start_key = jax.random.fold_in(key, 31)
    inside = jax.random.randint(start_key, (REPS, N_FSDP), 1, TOK_DEV, dtype=jnp.int32)
    blocks = jnp.arange(N_FSDP, dtype=jnp.int32)[None, :]
    inside = jnp.where(blocks == 0, jnp.int32(0), jnp.where(blocks == 1, jnp.int32(TOK_DEV - 1), inside))
    places = jnp.arange(TOK_DEV, dtype=jnp.int32)[None, None, :]
    block_ids = jnp.arange(N_FSDP, dtype=jnp.int32)[None, :, None]
    numbers = jnp.where(places >= inside[:, :, None], block_ids, block_ids - 1)
    return numbers.reshape(REPS, N_FSDP * TOK_DEV).astype(jnp.int32)


def strengthened(result, stream_key, source, target, parts, factor):
    owner, partner = [(jnp.arange(result.shape[dim]) // (result.shape[dim] // parts)).reshape([-1 if axis == dim else 1 for axis in range(result.ndim)]) for dim in (source, target)]
    chosen = jax.random.permutation(stream_key, parts)[partner]
    strong = (owner == chosen) | (owner == (partner + parts // 2) % parts)
    return jnp.where(strong, factor * result, result)


def block_scale(own_key, dims, shards, least, high):
    def one(dim, parts):
        steps = jax.random.uniform(jax.random.fold_in(jax.random.fold_in(own_key, 6), dim), (parts,), jnp.float32, least / len(shards), high / len(shards))
        return jnp.repeat(jnp.exp(steps), dims[dim] // parts).reshape((-1,) + (1,) * (len(dims) - dim - 1))

    gain = one(*shards[0])
    for cut in shards[1:]:
        gain = gain * one(*cut)
    return gain


def gaussian(rng, dims, spread, most, pieces=(), kind=jnp.bfloat16):
    gain = block_scale(rng, dims, pieces, -0.22, 0.18) if pieces else 1.0
    result = jax.random.normal(rng, dims, jnp.float32) * spread * gain
    return jnp.minimum(jnp.maximum(result, -most), most).astype(kind)


def noise_with(stream_key, dims, scale, limit, cuts, heavy, kind=jnp.bfloat16):
    result = scale * jax.random.normal(stream_key, dims, jnp.float32)
    if cuts:
        result = result * block_scale(stream_key, dims, cuts, -0.22, 0.18)
    return jnp.clip(strengthened(result, jax.random.fold_in(stream_key, 3), *heavy), -limit, limit).astype(kind)


def setup_inputs(seed: int = 0) -> dict:
    splits = jax.random.split(jax.random.key(seed), 9)
    activations = noise_with(splits[0], (REPS, TOKENS, DW), 1.0, 6.0, ((0, 4), (1, 8)), (1, 2, 8, 2.0))
    key_cotangent = gaussian(splits[1], (REPS, TOKENS, KVW), 2.0, 12.0, ((0, 4), (1, 8)))
    doc_ids = draw_doc_ids(jax.random.fold_in(splits[8], 71), 0)
    replica_params = draw_replica_params(jax.random.fold_in(splits[8], 71), 0)
    first_moment = gaussian(splits[4], (REPS, DW, KVW), 1.0, 6.0, ((0, 4), (1, 8)), jnp.float32)
    second_moment = jnp.clip(jnp.exp(math.log(16.0) - 2.7725887 * jax.random.uniform(splits[5], (REPS, DW, KVW), jnp.float32) ** block_scale(splits[5], (REPS, DW, KVW), ((0, 4), (1, 8)), -0.2, 0.2)), 1.0, 16.0)
    anchor = draw_anchor(jax.random.fold_in(splits[8], 71), 0)
    momentum = gaussian(splits[7], (DW, KVW), 0.5, 3.0, ((0, 32),), jnp.float32)
    return dict(activations=activations, key_cotangent=key_cotangent, doc_ids=doc_ids, replica_params=replica_params, first_moment=first_moment, second_moment=second_moment, anchor=anchor, momentum=momentum)


rope_base = 500000.0

def positions(doc_row):
    places = jnp.arange(doc_row.shape[0], dtype=jnp.int32)
    begins = jnp.concatenate([jnp.ones((1,), jnp.bool_), doc_row[1:] != doc_row[:-1]])
    run_start = lax.cummax(jnp.where(begins, places, jnp.int32(0)), axis=0)
    return (places - run_start).astype(jnp.float32)

def rotate_back(cotangent, offsets):
    row_count = cotangent.shape[0]
    half_head = HEAD // 2
    blocks = cotangent.astype(jnp.float32).reshape(row_count, KV_HEADS, 2, half_head)
    frequency = jnp.exp(jnp.arange(half_head, dtype=jnp.float32) * (-math.log(rope_base) / half_head))
    angles = offsets[:, None] * frequency[None, :]
    cosine = jnp.cos(angles)[:, None, :]
    sine_part = jnp.sin(angles)[:, None, :]
    lower_half = blocks[:, :, 0, :]
    upper_half = blocks[:, :, 1, :]
    fresh_lower = lower_half * cosine + upper_half * sine_part
    fresh_upper = upper_half * cosine - lower_half * sine_part
    return jnp.stack([fresh_lower, fresh_upper], axis=2).reshape(row_count, KV_HEADS * HEAD).astype(jnp.bfloat16)

def inner_step(grad, params, first, second):
    fresh_first = 0.9 * first + 0.1 * grad
    fresh_second = 0.95 * second + 0.05 * grad * grad
    stepped = params - 0.2 * (fresh_first / (jnp.sqrt(fresh_second) + 1e-08) + 0.1 * params)
    return (fresh_first, fresh_second, stepped)

def reference(activations, key_cotangent, doc_ids, replica_params, first_moment, second_moment, anchor, momentum):
    grad_scale = 1.0 / math.sqrt(TOKENS)

    def one_group(inputs):
        features, cotangent, doc_row, params, first, second = inputs
        rotated = rotate_back(cotangent, positions(doc_row))
        feature_blocks = features.reshape(N_FSDP, TOK_DEV, DW)
        rotated_blocks = rotated.reshape(N_FSDP, TOK_DEV, KV_HEADS * HEAD)

        def add_block(summed, pair):
            product = jnp.dot(pair[0].T, pair[1], preferred_element_type=jnp.float32) * grad_scale
            rounded = lax.optimization_barrier(product.astype(jnp.bfloat16))
            return (summed + rounded.astype(jnp.float32), None)
        grad = lax.scan(add_block, jnp.zeros((DW, KV_HEADS * HEAD), jnp.float32), (feature_blocks, rotated_blocks))[0]
        return inner_step(grad, params, first, second)
    new_first, new_second, stepped = lax.map(one_group, (activations, key_cotangent, doc_ids, replica_params, first_moment, second_moment))
    pseudo_grad = anchor - lax.optimization_barrier(jnp.sum(stepped, axis=0)) / N_REP
    new_momentum = 0.9 * momentum + pseudo_grad
    new_params = anchor - 0.7 * (pseudo_grad + 0.9 * new_momentum)
    return (new_first, new_second, new_momentum, new_params)
```

```python
import functools
import math

import jax
import jax.numpy as jnp
import numpy as np
from jax import lax
from jax.experimental import pallas as pl
from jax.experimental.pallas import tpu as pltpu
from jax.sharding import PartitionSpec as P

HEAD = 128
ROPE_BASE = 500000.0
HALVES = 2
F32, BF16 = jnp.float32, jnp.bfloat16
VMEM_LIMIT = 48 * 1024 * 1024


def schedule(line):
    order = np.zeros((line, line), np.int32)
    for z in range(line):
        when = {}
        for d in range(line):
            when[d] = line - d + z if d > z else (d + line - z if d < z else 10 * line)
        order[z] = sorted(range(line), key=lambda d: (when[d], abs(d - z) * -1))
    place = np.argsort(order, axis=1)
    sends = []
    for t in range(1, line):
        even, odd = [], []
        for z in range(line):
            right = line - t + z
            right = right if right < line else -1
            left = t - line + z
            left = left if left >= 0 else -1
            even.append(right if z % 2 == 0 else left)
            odd.append(left if z % 2 == 0 else right)
        sends.append((even, odd))
    return order, place, sends


def dot(a, b):
    return lax.dot_general(a, b, (((1,), (0,)), ((), ())), preferred_element_type=F32)


def rotate_kernel(row, doc_ref, prev_ref, cot_ref, *outs):
    tokens = doc_ref.shape[1]

    def start(doc):
        last = jnp.max(doc, axis=1, keepdims=True)
        return tokens - jnp.sum((doc == last).astype(jnp.int32), axis=1, keepdims=True)

    places = lax.broadcasted_iota(jnp.int32, (1, tokens), 1)
    own = start(doc_ref[...])
    before = start(prev_ref[...])
    offsets = jnp.where(places >= own, places - own, places + tokens - before).astype(F32)
    half = HEAD // 2
    steps = lax.broadcasted_iota(jnp.int32, (half, 1), 0).astype(F32)
    frequency = jnp.exp(steps * (-math.log(ROPE_BASE) / half))
    angles = frequency * offsets
    cosine, sine = jnp.cos(angles), jnp.sin(angles)
    width = outs[0].shape[0]
    for part, out in enumerate(outs):
        turned = cot_ref[:, part * width : (part + 1) * width].astype(F32).T
        for head in range(width // HEAD):
            low = turned[head * HEAD : head * HEAD + half]
            high = turned[head * HEAD + half : (head + 1) * HEAD]
            out[head * HEAD : head * HEAD + half, :] = (low * cosine + high * sine).astype(BF16)
            out[head * HEAD + half : (head + 1) * HEAD, :] = (high * cosine - low * sine).astype(BF16)


def send_kernel(cols, chunks, row, *refs):
    own, peer = refs[0], refs[1]
    at = 2
    streams = []
    for stream in cols:
        streams.append((stream, refs[at]))
        at += 1
    pieces = {}
    for k in chunks:
        pieces[k] = refs[at]
        at += 1
    befores = []
    for (slot, options, has_before), _ in streams:
        befores.append(refs[at] if has_before else None)
        at += int(has_before)
    outs = refs[at:]
    for ((slot, options, _), mine), before, out in zip(streams, befores, outs):
        valid, place = row[slot + 1], row[slot + 2]

        @pl.when(valid == 0)
        def _():
            out[...] = jnp.zeros_like(out)

        for k in options:

            @pl.when((valid == 1) & (place == k))
            def _():
                total = dot(own[...], mine[...]) + dot(peer[...], pieces[k][...])
                if before is not None:
                    total = total + before[...].astype(F32)
                out[...] = total.astype(BF16)


def final_kernel(scale, core_slot, row, *refs):
    own, peer, mine, theirs, even, odd, first, second = refs[:8]
    new_first, new_second, keep, give = refs[-4:]
    total = dot(own[...], mine[...]) + dot(peer[...], theirs[...])
    total = total + even[...].astype(F32) + odd[...].astype(F32)
    grad = total.T * scale
    fresh_first = 0.9 * first[...] + 0.1 * grad
    fresh_second = 0.95 * second[...] + 0.05 * grad * grad
    new_first[...] = fresh_first
    new_second[...] = fresh_second
    update = fresh_first / (jnp.sqrt(fresh_second) + 1e-08)
    count, share, width = keep.shape
    pairs = update.reshape(count, 2, share, width)
    zero = row[core_slot] == 0
    keep[...] = jnp.where(zero, pairs[:, 0], pairs[:, 1]).astype(keep.dtype)
    give[...] = jnp.where(zero, pairs[:, 1], pairs[:, 0]).astype(give.dtype)


def assemble_kernel(core_slot, row, mine, theirs, *refs):
    out = refs[-1]
    zero = row[core_slot] == 0
    a, b = mine[...], theirs[...]
    both = jnp.stack([jnp.where(zero, a, b), jnp.where(zero, b, a)], axis=1)
    out[...] = both.reshape(out.shape)


def call(kernel, row, grid, ins, outs, aliases=None):
    specs = []
    for array, block, index in ins:
        if index == "any":
            specs.append(pl.BlockSpec(memory_space=pl.ANY))
        elif block is None:
            rank = array.ndim
            specs.append(pl.BlockSpec(array.shape, functools.partial(lambda rank, i, s: (0,) * rank, rank)))
        else:
            specs.append(pl.BlockSpec(block, index))
    out_specs, shapes = [], []
    for shape, dtype, block, index in outs:
        rank = len(shape)
        shapes.append(jax.ShapeDtypeStruct(shape, dtype))
        if block is None:
            out_specs.append(pl.BlockSpec(shape, functools.partial(lambda rank, i, s: (0,) * rank, rank)))
        else:
            out_specs.append(pl.BlockSpec(block, index))
    return pl.pallas_call(
        kernel,
        grid_spec=pltpu.PrefetchScalarGridSpec(
            num_scalar_prefetch=1, grid=(grid,), in_specs=specs, out_specs=out_specs
        ),
        out_shape=shapes,
        input_output_aliases={k + 1: v for k, v in (aliases or {}).items()},
        compiler_params=pltpu.CompilerParams(vmem_limit_bytes=VMEM_LIMIT),
    )(row, *[array for array, _, _ in ins])


def local(fsdp, reps, activations, key_cotangent, doc_ids, replica_params, first_moment, second_moment, anchor, momentum):
    features, cotangent = activations[0], key_cotangent[0]
    params, first, second = replica_params[0], first_moment[0], second_moment[0]
    tokens, model = features.shape
    keys = cotangent.shape[1]
    rows = model // fsdp
    line = fsdp // 2
    share = anchor.shape[0]
    outer = reps // 2
    width = keys // HALVES
    order, place, sends = schedule(line)

    table, slots = [], {}
    for device in range(reps * fsdp):
        group, spot = divmod(device, fsdp)
        z, x = divmod(spot, 2)
        numbers = {"core": group % 2, "outer": group // 2}
        for k in range(line):
            numbers["pack", k] = 2 * order[z][k] + 1 - x
        numbers["own"] = 2 * z + x
        for t, streams in enumerate(sends, 1):
            for name, chunk in zip("eo", streams):
                d = chunk[z]
                numbers[name, t] = 2 * max(d, 0) + x
                numbers[name, t, "valid"] = int(d >= 0)
                numbers[name, t, "place"] = place[z][max(d, 0)]
        slots = {key: i for i, key in enumerate(numbers)}
        table.append([int(v) for v in numbers.values()])
    here = lax.axis_index("rep") * fsdp + lax.axis_index("fsdp")
    row = lax.dynamic_slice_in_dim(jnp.asarray(np.array(table, np.int32)), here, 1, 0)[0]
    core, out_spot = row[slots["core"]], row[slots["outer"]]

    pair = [(f, f ^ 1) for f in range(fsdp)]
    cores = [(r, r ^ 1) for r in range(reps)]
    across = [(r, r ^ 2) for r in range(reps)]
    evens, odds = [], []
    for z in range(line - 1):
        for x in range(2):
            a, b = 2 * z + x, 2 * z + 2 + x
            (evens if z % 2 == 0 else odds).extend([(a, b), (b, a)])

    prev = lax.ppermute(doc_ids, "fsdp", [(f, (f + 1) % fsdp) for f in range(fsdp)])

    def packed(k):
        return lax.dynamic_slice_in_dim(features, row[slots["pack", k]] * rows, rows, 1)

    pieces = [lax.ppermute(packed(0), "fsdp", pair)]
    own = call(
        rotate_kernel, row, 1, [(doc_ids, None, None), (prev, None, None), (cotangent, None, None)],
        [((width, tokens), BF16, None, None)] * HALVES,
    )
    peer = [lax.ppermute(part, "fsdp", pair) for part in own]
    for k in range(1, line):
        pieces.append(lax.ppermute(packed(k), "fsdp", pair))

    decay = 1.0 - 0.2 * 0.1
    groups = [[2 * q + c for q in range(outer)] for c in range(2)]
    split = params.reshape(outer, 2, share, keys)
    give = lax.dynamic_index_in_dim(split, 1 - core, 1, keepdims=False)
    stay = lax.dynamic_index_in_dim(split, core, 1, keepdims=False)
    held = stay + lax.ppermute(give, "rep", cores)
    if outer == 2:
        mine = lax.dynamic_index_in_dim(held, out_spot, 0, keepdims=False)
        other = lax.dynamic_index_in_dim(held, 1 - out_spot, 0, keepdims=False)
        summed = mine + lax.ppermute(other, "rep", across)
    else:
        summed = lax.psum_scatter(held, "rep", scatter_dimension=0, axis_index_groups=groups, tiled=False)
    base = anchor - (decay / reps) * summed
    momentum_base = 0.9 * momentum + base
    params_base = anchor - 0.7 * (base + 0.9 * momentum_base)
    if outer == 2:
        far = lax.ppermute(params_base, "rep", across)
        near = out_spot == 0
        bases = jnp.stack([jnp.where(near, params_base, far), jnp.where(near, far, params_base)])
    else:
        bases = lax.all_gather(params_base, "rep", axis_index_groups=groups)

    came = [(None, None)] * HALVES
    for t, streams in enumerate(sends, 1):
        for h in range(HALVES):
            cols, chunks, ins, outs = [], set(), [], []
            before = []
            for name, chunk, arrived in zip("eo", streams, came[h][::-1]):
                options = sorted({int(place[z][d]) for z, d in enumerate(chunk) if d >= 0 and 0 <= (z + (1 if (name == "e") == (z % 2 == 0) else -1)) < line})
                if not options:
                    continue
                chunks.update(options)
                cols.append((slots[name, t], options, arrived is not None))
                if arrived is not None:
                    before.append((arrived, None, None))
            ins = [(own[h], None, None), (peer[h], None, None)]
            for slot, _, _ in cols:
                ins.append((features, (tokens, rows), functools.partial(lambda slot, i, s: (0, s[slot]), slot)))
            ins += [(pieces[k], None, None) for k in sorted(chunks)] + before
            outs = [((width, rows), BF16, None, None)] * len(cols)
            sent = call(functools.partial(send_kernel, cols, sorted(chunks)), row, 1, ins, outs)
            even = lax.ppermute(sent[0], "fsdp", evens)
            odd = lax.ppermute(sent[1], "fsdp", odds) if len(sent) > 1 else None
            came[h] = (even, odd)

    scale = 1.0 / math.sqrt(tokens * fsdp)
    tall = max(2 * share, 128)
    steps = rows // tall
    new_first = new_second = new_params = None
    momenta = []
    for h in range(HALVES):
        even, odd = came[h]
        side = functools.partial(lambda h, i, s: (i, h), h)
        ins = [
            (own[h], None, None),
            (peer[h], None, None),
            (features, (tokens, tall), lambda i, s: (0, s[slots["own"]] * steps + i)),
            (pieces[line - 1], (tokens, tall), lambda i, s: (0, i)),
            (even, (width, tall), lambda i, s: (0, i)),
            (odd, (width, tall), lambda i, s: (0, i)),
            (first, (tall, width), side),
            (second, (tall, width), side),
        ]
        aliases = None
        if new_first is not None:
            ins += [(new_first, None, "any"), (new_second, None, "any")]
            aliases = {8: 0, 9: 1}
        each = tall // (2 * share)
        new_first, new_second, keep, give = call(
            functools.partial(final_kernel, scale, slots["core"]), row, steps, ins,
            [
                ((rows, keys), F32, (tall, width), side),
                ((rows, keys), F32, (tall, width), side),
                ((outer, share, width), F32, (each, share, width), lambda i, s: (i, 0, 0)),
                ((outer, share, width), BF16, (each, share, width), lambda i, s: (i, 0, 0)),
            ],
            aliases,
        )
        both = keep + lax.ppermute(give, "rep", cores).astype(F32)
        if outer == 2:
            both = both.astype(BF16)
            total = both.astype(F32) + lax.ppermute(both, "rep", across).astype(F32)
        else:
            total = lax.psum(both, "rep", axis_index_groups=groups)
        part = slice(h * width, (h + 1) * width)
        mean = (0.2 / reps) * total
        momenta.append(momentum_base[:, part] + lax.dynamic_index_in_dim(mean, out_spot, 0, keepdims=False))
        fresh = bases[:, :, part] - (0.7 * 1.9) * mean
        theirs = lax.ppermute(fresh, "rep", cores)
        ins = [(fresh, None, None), (theirs, None, None)]
        aliases = None
        if new_params is not None:
            ins.append((new_params, None, "any"))
            aliases = {2: 0}
        (new_params,) = call(
            functools.partial(assemble_kernel, slots["core"]), row, 1, ins,
            [((rows, keys), F32, (rows, width), functools.partial(lambda h, i, s: (0, h), h))],
            aliases,
        )
    new_momentum = jnp.concatenate(momenta, axis=1)
    return (new_first[None], new_second[None], new_momentum, new_params)


def solution(mesh):
    fsdp, reps = mesh.shape["fsdp"], mesh.shape["rep"]
    placed = (
        P("rep", "fsdp", None),
        P("rep", "fsdp", None),
        P("rep", "fsdp"),
        P("rep", "fsdp", None),
        P("rep", "fsdp", None),
        P("rep", "fsdp", None),
        P(("fsdp", "rep"), None),
        P(("fsdp", "rep"), None),
    )
    return jax.shard_map(
        functools.partial(local, fsdp, reps),
        mesh=mesh,
        in_specs=placed,
        out_specs=(
            P("rep", "fsdp", None),
            P("rep", "fsdp", None),
            P(("fsdp", "rep"), None),
            P("fsdp", None),
        ),
        check_vma=False,
    )
```

```python
import functools
import math

import jax
import jax.numpy as jnp
import numpy as np
from jax import lax
from jax.experimental import pallas as pl
from jax.experimental.pallas import tpu as pltpu
from jax.sharding import PartitionSpec as P

HEAD = 128
ROPE_BASE = 500000.0
HALVES = 2
F32, BF16 = jnp.float32, jnp.bfloat16
VMEM_LIMIT = 16 * 1024 * 1024


def schedule(line):
    order = np.zeros((line, line), np.int32)
    for z in range(line):
        when = {}
        for d in range(line):
            when[d] = line - d + z if d > z else (d + line - z if d < z else 10 * line)
        order[z] = sorted(range(line), key=lambda d: (when[d], abs(d - z) * -1))
    place = np.argsort(order, axis=1)
    sends = []
    for t in range(1, line):
        even, odd = [], []
        for z in range(line):
            right = line - t + z
            right = right if right < line else -1
            left = t - line + z
            left = left if left >= 0 else -1
            even.append(right if z % 2 == 0 else left)
            odd.append(left if z % 2 == 0 else right)
        sends.append((even, odd))
    return order, place, sends


def dot(a, b):
    return lax.dot_general(a, b, (((1,), (0,)), ((), ())), preferred_element_type=F32)


def spot():
    here = lax.axis_index("fsdp")
    return lax.div(here, 2), lax.rem(here, 2)


def pick(index, values):
    total = jnp.int32(0)
    for i, value in enumerate(values):
        if value:
            total = total + jnp.where(index == i, jnp.int32(value), 0)
    return total


def columns(chunk, side, rows):
    return pl.ds(pl.multiple_of((2 * chunk + side) * rows, rows), rows)


def pack_kernel(order, which, features, *refs):
    z, x = spot()
    outs, sems = refs[:-1], refs[-1]
    rows = outs[0].shape[1]
    copies = []
    for i, (k, out) in enumerate(zip(which, outs)):
        chunk = pick(z, [int(order[p][k]) for p in range(len(order))])
        copies.append(pltpu.make_async_copy(features.at[:, columns(chunk, 1 - x, rows)], out, sems.at[i]))
    for copy in copies:
        copy.start()
    for copy in copies:
        copy.wait()


def rotate_kernel(doc_ref, prev_ref, cot_ref, *outs):
    tokens = doc_ref.shape[1]

    def start(doc):
        last = jnp.max(doc, axis=1, keepdims=True)
        return tokens - jnp.sum((doc == last).astype(jnp.int32), axis=1, keepdims=True)

    places = lax.broadcasted_iota(jnp.int32, (1, tokens), 1)
    own = start(doc_ref[...])
    before = start(prev_ref[...])
    offsets = jnp.where(places >= own, places - own, places + tokens - before).astype(F32)
    half = HEAD // 2
    steps = lax.broadcasted_iota(jnp.int32, (half, 1), 0).astype(F32)
    frequency = jnp.exp(steps * (-math.log(ROPE_BASE) / half))
    angles = frequency * offsets
    cosine, sine = jnp.cos(angles), jnp.sin(angles)
    width = outs[0].shape[0]
    for part, out in enumerate(outs):
        turned = cot_ref[:, part * width : (part + 1) * width].astype(F32).T
        for head in range(width // HEAD):
            low = turned[head * HEAD : head * HEAD + half]
            high = turned[head * HEAD + half : (head + 1) * HEAD]
            out[head * HEAD : head * HEAD + half, :] = (low * cosine + high * sine).astype(BF16)
            out[head * HEAD + half : (head + 1) * HEAD, :] = (high * cosine - low * sine).astype(BF16)


def send_kernel(line, streams, chunks, own, peer, features, *refs):
    z, x = spot()
    pieces = dict(zip(chunks, refs))
    befores = refs[len(chunks) : len(refs) - len(streams)]
    outs = refs[len(refs) - len(streams) :]
    at = 0
    for (chunk, place, options, has_before), out in zip(streams, outs):
        rows = out.shape[1]
        before = befores[at] if has_before else None
        at += int(has_before)
        valid = pick(z, [int(d >= 0) for d in chunk])
        where = pick(z, place)
        mine = columns(pick(z, [max(d, 0) for d in chunk]), x, rows)

        @pl.when(valid == 0)
        def _():
            out[...] = jnp.zeros_like(out)

        for k in options:

            @pl.when((valid == 1) & (where == k))
            def _():
                total = dot(own[...], features[:, mine]) + dot(peer[...], pieces[k][...])
                if before is not None:
                    total = total + before[...].astype(F32)
                out[...] = total.astype(BF16)


def final_kernel(scale, part, own, peer, features, theirs, even, odd, first, second, *refs):
    new_first, new_second, keep, give = refs[-4:]
    z, x = spot()
    rows = theirs.shape[1]
    count, share, width = keep.shape
    total = dot(own[...], features[:, columns(z, x, rows)]) + dot(peer[...], theirs[...])
    total = total + even[...].astype(F32) + odd[...].astype(F32)
    grad = total.T * scale
    cols = slice(part * width, (part + 1) * width)
    fresh_first = 0.9 * first[:, cols] + 0.1 * grad
    fresh_second = 0.95 * second[:, cols] + 0.05 * grad * grad
    new_first[...] = fresh_first
    new_second[...] = fresh_second
    update = fresh_first / (jnp.sqrt(fresh_second) + 1e-08)
    ours, theirs = halves(update, count, share)
    keep[...] = ours.astype(keep.dtype)
    give[...] = theirs.astype(give.dtype)


def halves(value, count, share):
    pairs = value.reshape(count, 2, share, value.shape[-1])
    zero = lax.rem(lax.axis_index("rep"), 2) == 0
    return jnp.where(zero, pairs[:, 0], pairs[:, 1]), jnp.where(zero, pairs[:, 1], pairs[:, 0])


def split_kernel(params, stay, give):
    count, share, _ = stay.shape
    stay[...], give[...] = halves(params[...], count, share)


def partial_kernel(stay, came, mine, other):
    near = lax.div(lax.axis_index("rep"), 2) == 0
    held = stay[...] + came[...]
    mine[...] = jnp.where(near, held[0], held[1])
    other[...] = jnp.where(near, held[1], held[0])


def outer_kernel(part, reps, both, came, params_base, far_base, momentum_base, *refs):
    momentum, fresh = refs[-2:]
    near = lax.div(lax.axis_index("rep"), 2) == 0
    mean = (both[...].astype(F32) + came[...].astype(F32)) * (0.2 / reps)
    width = mean.shape[-1]
    cols = slice(part * width, (part + 1) * width)
    mine, far = params_base[:, cols], far_base[:, cols]
    fresh[0] = jnp.where(near, mine, far) - (0.7 * 1.9) * mean[0]
    fresh[1] = jnp.where(near, far, mine) - (0.7 * 1.9) * mean[1]
    momentum[...] = momentum_base[:, cols] + jnp.where(near, mean[0], mean[1])


def assemble_kernel(mine, theirs, *refs):
    out = refs[-1]
    zero = lax.rem(lax.axis_index("rep"), 2) == 0
    a, b = mine[...], theirs[...]
    both = jnp.stack([jnp.where(zero, a, b), jnp.where(zero, b, a)], axis=1)
    out[...] = both.reshape(out.shape)


def after(value, *others):
    return lax.optimization_barrier((value, *others))[0]


def call(kernel, ins, outs, scratch=(), into=None, places=None):
    into = into or []
    spaces = list(places or [pltpu.VMEM] * len(ins)) + [pl.ANY] * len(into)
    out_specs, shapes = [], []
    for shape, dtype, *block in outs:
        shapes.append(jax.ShapeDtypeStruct(shape, dtype))
        if block:
            out_specs.append(pl.BlockSpec((shape[0], block[1]), functools.partial(lambda part, i: (0, part), block[0])))
        else:
            out_specs.append(pl.BlockSpec(memory_space=pltpu.VMEM))
    return pl.pallas_call(
        kernel,
        grid=(1,),
        in_specs=[pl.BlockSpec(memory_space=space) for space in spaces],
        out_specs=out_specs,
        out_shape=shapes,
        scratch_shapes=list(scratch),
        input_output_aliases={len(ins) + i: i for i in range(len(into))},
        compiler_params=pltpu.CompilerParams(vmem_limit_bytes=VMEM_LIMIT),
    )(*ins, *into)


def local(fsdp, reps, activations, key_cotangent, doc_ids, replica_params, first_moment, second_moment, anchor, momentum):
    features, cotangent = activations[0], key_cotangent[0]
    params, first, second = replica_params[0], first_moment[0], second_moment[0]
    tokens, model = features.shape
    keys = cotangent.shape[1]
    rows = model // fsdp
    line = fsdp // 2
    share = anchor.shape[0]
    outer = reps // 2
    width = keys // HALVES
    order, place, sends = schedule(line)

    pair = [(f, f ^ 1) for f in range(fsdp)]
    cores = [(r, r ^ 1) for r in range(reps)]
    across = [(r, r ^ 2) for r in range(reps)]
    evens, odds = [], []
    for z in range(line - 1):
        for x in range(2):
            a, b = 2 * z + x, 2 * z + 2 + x
            (evens if z % 2 == 0 else odds).extend([(a, b), (b, a)])

    prev = lax.ppermute(doc_ids, "fsdp", [(f, f + 1) for f in range(fsdp - 1)])

    def packed(source, which):
        return call(
            functools.partial(pack_kernel, order, which), [source],
            [((tokens, rows), BF16)] * len(which),
            scratch=[pltpu.SemaphoreType.DMA((len(which),))], places=[pl.ANY],
        )

    pieces = [lax.ppermute(after(packed(features, [0])[0], prev), "fsdp", pair)]
    own = list(call(rotate_kernel, [doc_ids, prev, cotangent], [((width, tokens), BF16)] * HALVES))
    peer = [lax.ppermute(part, "fsdp", pair) for part in own]
    pieces += [lax.ppermute(piece, "fsdp", pair) for piece in packed(features, list(range(1, line)))]

    decay = 1.0 - 0.2 * 0.1
    groups = [[2 * q + c for q in range(outer)] for c in range(2)]
    block = ((outer, share, keys), F32)
    stay, give = call(split_kernel, [after(params, own[0])], [block] * 2)
    crossed = lax.ppermute(give, "rep", cores)
    ready = None
    if outer == 2:
        mine, ready = call(partial_kernel, [stay, crossed], [((share, keys), F32)] * 2)
        summed = mine + lax.ppermute(ready, "rep", across)
    else:
        summed = lax.psum_scatter(stay + crossed, "rep", scatter_dimension=0, axis_index_groups=groups, tiled=False)
    base = anchor - (decay / reps) * summed
    momentum_base = 0.9 * momentum + base
    params_base = anchor - 0.7 * (base + 0.9 * momentum_base)
    if outer == 2:
        far_base = lax.ppermute(params_base, "rep", across)
    else:
        bases = lax.all_gather(params_base, "rep", axis_index_groups=groups)

    came = [(None, None)] * HALVES
    for t, streams in enumerate(sends, 1):
        for h in range(HALVES):
            kept, chunks, before = [], set(), []
            for chunk, arrived in zip(streams, came[h][::-1]):
                options = sorted({int(place[z][d]) for z, d in enumerate(chunk) if d >= 0})
                if not options:
                    continue
                chunks.update(options)
                kept.append((chunk, [int(place[z][max(d, 0)]) for z, d in enumerate(chunk)], options, arrived is not None))
                if arrived is not None:
                    before.append(arrived)
            if outer == 2 and h == 0:
                if t == 2:
                    own[h] = after(own[h], ready)
                if t == 3:
                    own[h] = after(own[h], params_base)
            sent = call(
                functools.partial(send_kernel, line, kept, sorted(chunks)),
                [own[h], peer[h], features] + [pieces[k] for k in sorted(chunks)] + before,
                [((width, rows), BF16)] * len(kept),
            )
            even = lax.ppermute(sent[0], "fsdp", evens)
            odd = lax.ppermute(sent[1], "fsdp", odds) if len(sent) > 1 else None
            came[h] = (even, odd)

    scale = 1.0 / math.sqrt(tokens * fsdp)
    new_first = new_second = new_params = new_momentum = None
    momenta = []
    for h in range(HALVES):
        ins = [own[h], peer[h], features, pieces[line - 1], *came[h], first, second]
        new_first, new_second, keep, give = call(
            functools.partial(final_kernel, scale, h), ins,
            [((rows, keys), F32, h, width)] * 2 + [((outer, share, width), BF16)] * 2,
            into=[new_first, new_second] if h else None,
        )
        both = keep.astype(F32) + lax.ppermute(give, "rep", cores).astype(F32)
        if outer == 2:
            both = both.astype(BF16)
            ins = [both, lax.ppermute(both, "rep", across), params_base, far_base, momentum_base]
            new_momentum, fresh = call(
                functools.partial(outer_kernel, h, reps), ins,
                [((share, keys), F32, h, width), ((outer, share, width), F32)],
                into=[new_momentum] if h else None,
            )
        else:
            part = slice(h * width, (h + 1) * width)
            mean = (0.2 / reps) * lax.psum(both, "rep", axis_index_groups=groups)
            mine = lax.dynamic_index_in_dim(mean, lax.div(lax.axis_index("rep"), 2), 0, keepdims=False)
            momenta.append(momentum_base[:, part] + mine)
            fresh = bases[:, :, part] - (0.7 * 1.9) * mean
        ins = [fresh, lax.ppermute(fresh, "rep", cores)]
        (new_params,) = call(
            assemble_kernel, ins, [((rows, keys), F32, h, width)],
            into=[new_params] if h else None,
        )
    if outer != 2:
        new_momentum = jnp.concatenate(momenta, axis=1)
    return (new_first[None], new_second[None], new_momentum, new_params)


def solution(mesh):
    fsdp, reps = mesh.shape["fsdp"], mesh.shape["rep"]
    placed = (
        P("rep", "fsdp", None),
        P("rep", "fsdp", None),
        P("rep", "fsdp"),
        P("rep", "fsdp", None),
        P("rep", "fsdp", None),
        P("rep", "fsdp", None),
        P(("fsdp", "rep"), None),
        P(("fsdp", "rep"), None),
    )
    return jax.shard_map(
        functools.partial(local, fsdp, reps),
        mesh=mesh,
        in_specs=placed,
        out_specs=(
            P("rep", "fsdp", None),
            P("rep", "fsdp", None),
            P(("fsdp", "rep"), None),
            P("fsdp", None),
        ),
        check_vma=False,
    )
```

```python
import functools
import math

import jax
import jax.numpy as jnp
import numpy as np
from jax import lax
from jax.experimental import pallas as pl
from jax.experimental.pallas import tpu as pltpu
from jax.sharding import PartitionSpec as P

HEAD = 128
ROPE_BASE = 500000.0
HALVES = 2
F32, BF16 = jnp.float32, jnp.bfloat16
VMEM_LIMIT = 16 * 1024 * 1024


def schedule(line):
    order = np.zeros((line, line), np.int32)
    for z in range(line):
        when = {}
        for d in range(line):
            when[d] = line - d + z if d > z else (d + line - z if d < z else 10 * line)
        order[z] = sorted(range(line), key=lambda d: (when[d], abs(d - z) * -1))
    place = np.argsort(order, axis=1)
    sends = []
    for t in range(1, line):
        even, odd = [], []
        for z in range(line):
            right = line - t + z
            right = right if right < line else -1
            left = t - line + z
            left = left if left >= 0 else -1
            even.append(right if z % 2 == 0 else left)
            odd.append(left if z % 2 == 0 else right)
        sends.append((even, odd))
    return order, place, sends


def dot(a, b):
    return lax.dot_general(a, b, (((1,), (0,)), ((), ())), preferred_element_type=F32)


def spot():
    here = lax.axis_index("fsdp")
    return lax.div(here, 2), lax.rem(here, 2)


def pick(index, values):
    total = jnp.int32(0)
    for i, value in enumerate(values):
        if value:
            total = total + jnp.where(index == i, jnp.int32(value), 0)
    return total


def columns(chunk, side, rows):
    return pl.ds(pl.multiple_of((2 * chunk + side) * rows, rows), rows)


def pack_kernel(order, which, features, *refs):
    z, x = spot()
    outs, sems = refs[:-1], refs[-1]
    rows = outs[0].shape[1]
    copies = []
    for i, (k, out) in enumerate(zip(which, outs)):
        chunk = pick(z, [int(order[p][k]) for p in range(len(order))])
        copies.append(pltpu.make_async_copy(features.at[:, columns(chunk, 1 - x, rows)], out, sems.at[i]))
    for copy in copies:
        copy.start()
    for copy in copies:
        copy.wait()


def rotate_kernel(doc_ref, prev_ref, cot_ref, *outs):
    tokens = doc_ref.shape[1]

    def start(doc):
        last = jnp.max(doc, axis=1, keepdims=True)
        return tokens - jnp.sum((doc == last).astype(jnp.int32), axis=1, keepdims=True)

    places = lax.broadcasted_iota(jnp.int32, (1, tokens), 1)
    own = start(doc_ref[...])
    before = start(prev_ref[...])
    offsets = jnp.where(places >= own, places - own, places + tokens - before).astype(F32)
    half = HEAD // 2
    steps = lax.broadcasted_iota(jnp.int32, (half, 1), 0).astype(F32)
    frequency = jnp.exp(steps * (-math.log(ROPE_BASE) / half))
    angles = frequency * offsets
    cosine, sine = jnp.cos(angles), jnp.sin(angles)
    width = outs[0].shape[0]
    for part, out in enumerate(outs):
        turned = cot_ref[:, part * width : (part + 1) * width].astype(F32).T
        for head in range(width // HEAD):
            low = turned[head * HEAD : head * HEAD + half]
            high = turned[head * HEAD + half : (head + 1) * HEAD]
            out[head * HEAD : head * HEAD + half, :] = (low * cosine + high * sine).astype(BF16)
            out[head * HEAD + half : (head + 1) * HEAD, :] = (high * cosine - low * sine).astype(BF16)


def send_kernel(chunk, place, options, own, peer, features, *refs):
    z, x = spot()
    pieces = dict(zip(options, refs))
    befores, out = refs[len(options) : -1], refs[-1]
    valid = pick(z, [int(d >= 0) for d in chunk])
    where = pick(z, place)
    mine = columns(pick(z, [max(d, 0) for d in chunk]), x, out.shape[1])

    @pl.when(valid == 0)
    def _():
        out[...] = jnp.zeros_like(out)

    for k in options:

        @pl.when((valid == 1) & (where == k))
        def _():
            total = dot(own[...], features[:, mine]) + dot(peer[...], pieces[k][...])
            for before in befores:
                total = total + before[...].astype(F32)
            out[...] = total.astype(BF16)


def own_kernel(own, peer, features, theirs, out):
    z, x = spot()
    out[...] = dot(own[...], features[:, columns(z, x, theirs.shape[1])]) + dot(peer[...], theirs[...])


def inner(scale, cols, total, even, odd, first, second):
    grad = (total[...] + even[...].astype(F32) + odd[...].astype(F32)).T * scale
    fresh_first = 0.9 * first[:, cols] + 0.1 * grad
    fresh_second = 0.95 * second[:, cols] + 0.05 * grad * grad
    return fresh_first, fresh_second


def update_kernel(scale, cols, total, even, odd, first, second, keep, give):
    fresh_first, fresh_second = inner(scale, cols, total, even, odd, first, second)
    count, share, _ = keep.shape
    ours, theirs = halves(fresh_first / (jnp.sqrt(fresh_second) + 1e-08), count, share)
    keep[...] = ours.astype(keep.dtype)
    give[...] = theirs.astype(give.dtype)


def moments_kernel(scale, cols, total, even, odd, first, second, *refs):
    new_first, new_second, done = refs[-3:]
    new_first[...], new_second[...] = inner(scale, cols, total, even, odd, first, second)
    done[...] = jnp.zeros_like(done)


def halves(value, count, share):
    pairs = value.reshape(count, 2, share, value.shape[-1])
    zero = lax.rem(lax.axis_index("rep"), 2) == 0
    return jnp.where(zero, pairs[:, 0], pairs[:, 1]), jnp.where(zero, pairs[:, 1], pairs[:, 0])


def held_kernel(params, came, out):
    count, share, _ = out.shape
    out[...] = halves(params[...], count, share)[0] + halves(came[...], count, share)[0]


def partial_kernel(params, came, mine, other):
    share = mine.shape[0]
    core, near = lax.rem(lax.axis_index("rep"), 2), lax.div(lax.axis_index("rep"), 2)

    def block(at):
        part = pl.ds(pl.multiple_of((2 * at + core) * share, share), share)
        return params[part, :] + came[part, :]

    mine[...] = block(near)
    other[...] = block(1 - near)


def outer_kernel(part, reps, both, came, params_base, far_base, momentum_base, *refs):
    momentum, fresh = refs[-2:]
    near = lax.div(lax.axis_index("rep"), 2) == 0
    mean = (both[...].astype(F32) + came[...].astype(F32)) * (0.2 / reps)
    width = mean.shape[-1]
    cols = slice(part * width, (part + 1) * width)
    mine, far = params_base[:, cols], far_base[:, cols]
    fresh[0] = jnp.where(near, mine, far) - (0.7 * 1.9) * mean[0]
    fresh[1] = jnp.where(near, far, mine) - (0.7 * 1.9) * mean[1]
    momentum[...] = momentum_base[:, cols] + jnp.where(near, mean[0], mean[1])


def assemble_kernel(mine, theirs, *refs):
    out = refs[-1]
    zero = lax.rem(lax.axis_index("rep"), 2) == 0
    a, b = mine[...], theirs[...]
    both = jnp.stack([jnp.where(zero, a, b), jnp.where(zero, b, a)], axis=1)
    out[...] = both.reshape(out.shape)


def here(value):
    return pltpu.with_memory_space_constraint(value, pltpu.HBM)


def after(value, *others):
    return lax.optimization_barrier((value, *others))[0]


def call(kernel, ins, outs, scratch=(), into=None, places=None, cost=1):
    into = into or []
    spaces = list(places or [pltpu.VMEM] * len(ins)) + [pl.ANY] * len(into)
    out_specs, shapes = [], []
    for shape, dtype, *block in outs:
        shapes.append(jax.ShapeDtypeStruct(shape, dtype))
        if block:
            out_specs.append(pl.BlockSpec((shape[0], block[1]), functools.partial(lambda part, i: (0, part), block[0])))
        else:
            out_specs.append(pl.BlockSpec(memory_space=pltpu.VMEM))
    return pl.pallas_call(
        kernel,
        grid=(1,),
        in_specs=[pl.BlockSpec(memory_space=space) for space in spaces],
        out_specs=out_specs,
        out_shape=shapes,
        scratch_shapes=list(scratch),
        input_output_aliases={len(ins) + i: i for i in range(len(into))},
        cost_estimate=pl.CostEstimate(flops=1, transcendentals=0, bytes_accessed=cost),
        compiler_params=pltpu.CompilerParams(vmem_limit_bytes=VMEM_LIMIT),
    )(*ins, *into)


def local(fsdp, reps, activations, key_cotangent, doc_ids, replica_params, first_moment, second_moment, anchor, momentum):
    features, cotangent = activations[0], key_cotangent[0]
    params, first, second = replica_params[0], first_moment[0], second_moment[0]
    tokens, model = features.shape
    keys = cotangent.shape[1]
    rows = model // fsdp
    line = fsdp // 2
    share = anchor.shape[0]
    outer = reps // 2
    width = keys // HALVES
    order, place, sends = schedule(line)

    pair = [(f, f ^ 1) for f in range(fsdp)]
    cores = [(r, r ^ 1) for r in range(reps)]
    across = [(r, r ^ 2) for r in range(reps)]
    evens, odds = [], []
    for z in range(line - 1):
        for x in range(2):
            a, b = 2 * z + x, 2 * z + 2 + x
            (evens if z % 2 == 0 else odds).extend([(a, b), (b, a)])

    prev = lax.ppermute(doc_ids, "fsdp", [(f, f + 1) for f in range(fsdp - 1)])

    def packed(source, which):
        return call(
            functools.partial(pack_kernel, order, which), [here(source)],
            [((tokens, rows), BF16)] * len(which),
            scratch=[pltpu.SemaphoreType.DMA((len(which),))], places=[pltpu.HBM],
        )

    (first_piece,) = packed(features, [0])
    pieces = [lax.ppermute(first_piece, "fsdp", pair)]

    decay = 1.0 - 0.2 * 0.1
    groups = [[2 * q + c for q in range(outer)] for c in range(2)]
    block = ((outer, share, keys), F32)
    crossed = lax.ppermute(params, "rep", cores)
    if outer == 2:
        mine, ready = call(partial_kernel, [params, crossed], [((share, keys), F32)] * 2)
        summed = mine + lax.ppermute(ready, "rep", across)
    else:
        (held,) = call(held_kernel, [params, crossed], [block])
        summed = lax.psum_scatter(held, "rep", scatter_dimension=0, axis_index_groups=groups, tiled=False)
    own = list(call(rotate_kernel, [here(doc_ids), prev, after(cotangent, pieces[0])], [((width, tokens), BF16)] * HALVES))
    peer = [lax.ppermute(part, "fsdp", pair) for part in own]
    later = packed(features, list(range(1, line)))

    def exchange(k, *done):
        pieces.append(lax.ppermute(after(later[k - 1], *done), "fsdp", pair))

    exchange(1)
    if line > 2:
        exchange(2, peer[0])

    base = anchor - (decay / reps) * summed
    momentum_base = 0.9 * momentum + base
    params_base = anchor - 0.7 * (base + 0.9 * momentum_base)
    if outer == 2:
        far_base = lax.ppermute(params_base, "rep", across)
    else:
        bases = lax.all_gather(params_base, "rep", axis_index_groups=groups)

    came = [[None, None] for _ in range(HALVES)]
    for t, streams in enumerate(sends, 1):
        arrived = [half[::-1] for half in came]
        sent = {}
        for side in (1, 0) if t == 2 else (0, 1):
            chunk = streams[side]
            options = sorted({int(place[z][d]) for z, d in enumerate(chunk) if d >= 0})
            if not options:
                continue
            spots = [int(place[z][max(d, 0)]) for z, d in enumerate(chunk)]
            for h in range(HALVES):
                mine = own[h]
                if (t, side) == (2, 0):
                    mine = after(mine, *sent.values())
                if (t, side, h) == (3, 0, 0):
                    mine = after(mine, arrived[1][0])
                if outer == 2 and (side, h) == (0, 0):
                    mine = after(mine, *([ready] if t == 1 else [far_base] if t == 2 else []))
                if outer == 2 and (t, side, h) == (2, 1, 0):
                    mine = after(mine, params_base)
                before = [] if arrived[h][side] is None else [arrived[h][side]]
                (sent[side, h],) = call(
                    functools.partial(send_kernel, chunk, spots, options),
                    [mine, peer[h], features] + [pieces[k] for k in options] + before,
                    [((width, rows), BF16)],
                )
                came[h][side] = lax.ppermute(sent[side, h], "fsdp", odds if side else evens)
        if 2 <= t < line - 1:
            exchange(t + 1, sent[0, 0])

    scale = 1.0 / math.sqrt(tokens * fsdp)
    new_first = new_second = new_params = new_momentum = None
    momenta, tokens_done = [], []
    for h in range(HALVES):
        cols = slice(h * width, (h + 1) * width)
        mine = after(own[h], *sent.values()) if h == 0 else own[h]
        (total,) = call(own_kernel, [mine, peer[h], features, pieces[line - 1]], [((width, rows), F32)])
        if outer == 2:
            total = after(total, far_base)
        keep, give = call(
            functools.partial(update_kernel, scale, cols), [total, *came[h], first, second],
            [((outer, share, width), BF16)] * 2,
        )
        both = keep.astype(F32) + lax.ppermute(give, "rep", cores).astype(F32)
        if outer == 2:
            both = both.astype(BF16)
        new_first, new_second, done = call(
            functools.partial(moments_kernel, scale, cols), [after(total, both), *came[h], first, second],
            [((rows, keys), F32, h, width)] * 2 + [((8, 128), F32)], into=[new_first, new_second] if h else None,
            cost=3 * rows * keys * 4,
        )
        tokens_done.append(done)
        if outer == 2:
            ins = [both if h == 0 else after(both, *tokens_done), lax.ppermute(both, "rep", across), params_base, far_base, momentum_base]
            new_momentum, fresh = call(
                functools.partial(outer_kernel, h, reps), ins,
                [((share, keys), F32, h, width), ((outer, share, width), F32)],
                into=[new_momentum] if h else None,
            )
        else:
            part = slice(h * width, (h + 1) * width)
            mean = (0.2 / reps) * lax.psum(both, "rep", axis_index_groups=groups)
            mine = lax.dynamic_index_in_dim(mean, lax.div(lax.axis_index("rep"), 2), 0, keepdims=False)
            momenta.append(momentum_base[:, part] + mine)
            fresh = bases[:, :, part] - (0.7 * 1.9) * mean
        ins = [fresh, lax.ppermute(fresh, "rep", cores)]
        (new_params,) = call(
            assemble_kernel, ins, [((rows, keys), F32, h, width)],
            into=[new_params] if h else None,
        )
    if outer != 2:
        new_momentum = jnp.concatenate(momenta, axis=1)
    return (new_first[None], new_second[None], new_momentum, new_params)


def solution(mesh):
    fsdp, reps = mesh.shape["fsdp"], mesh.shape["rep"]
    placed = (
        P("rep", "fsdp", None),
        P("rep", "fsdp", None),
        P("rep", "fsdp"),
        P("rep", "fsdp", None),
        P("rep", "fsdp", None),
        P("rep", "fsdp", None),
        P(("fsdp", "rep"), None),
        P(("fsdp", "rep"), None),
    )
    return jax.shard_map(
        functools.partial(local, fsdp, reps),
        mesh=mesh,
        in_specs=placed,
        out_specs=(
            P("rep", "fsdp", None),
            P("rep", "fsdp", None),
            P(("fsdp", "rep"), None),
            P("fsdp", None),
        ),
        check_vma=False,
    )
```

```python
import functools
import math

import jax
import jax.numpy as jnp
import numpy as np
from jax import lax
from jax.experimental import pallas as pl
from jax.experimental.pallas import tpu as pltpu
from jax.sharding import PartitionSpec as P

HEAD = 128
ROPE_BASE = 500000.0
HALVES = 2
F32, BF16 = jnp.float32, jnp.bfloat16
VMEM_LIMIT = 16 * 1024 * 1024


def schedule(line):
    order = np.zeros((line, line), np.int32)
    for z in range(line):
        when = {}
        for d in range(line):
            when[d] = line - d + z if d > z else (d + line - z if d < z else 10 * line)
        order[z] = sorted(range(line), key=lambda d: (when[d], abs(d - z) * -1))
    place = np.argsort(order, axis=1)
    sends = []
    for t in range(1, line):
        even, odd = [], []
        for z in range(line):
            right = line - t + z
            right = right if right < line else -1
            left = t - line + z
            left = left if left >= 0 else -1
            even.append(right if z % 2 == 0 else left)
            odd.append(left if z % 2 == 0 else right)
        sends.append((even, odd))
    return order, place, sends


def dot(a, b):
    return lax.dot_general(a, b, (((1,), (0,)), ((), ())), preferred_element_type=F32)


def spot():
    here = lax.axis_index("fsdp")
    return lax.div(here, 2), lax.rem(here, 2)


def pick(index, values):
    total = jnp.int32(0)
    for i, value in enumerate(values):
        if value:
            total = total + jnp.where(index == i, jnp.int32(value), 0)
    return total


def columns(chunk, side, rows):
    return pl.ds(pl.multiple_of((2 * chunk + side) * rows, rows), rows)


def pack_kernel(order, which, features, *refs):
    z, x = spot()
    sems = refs[-1]
    source, outs = (refs[0], refs[1:-1]) if which == [0] else (None, refs[:-1])
    rows = features.shape[1] // (2 * len(order))
    moves = []
    for k, out in zip(which, outs):
        chunk = pick(z, [int(order[p][k]) for p in range(len(order))])
        moves.append((features.at[:, columns(chunk, 1 - x, rows)], out.at[:, :rows]))
    if source is not None:
        width = source.shape[1] // len(outs)
        for at, out in enumerate(outs):
            target = out.at[:, rows:] if at == 0 else out
            moves.append((source.at[:, at * width : (at + 1) * width], target))
    copies = [pltpu.make_async_copy(*move, sems.at[i]) for i, move in enumerate(moves)]
    for copy in copies:
        copy.start()
    for copy in copies:
        copy.wait()


def turn(cosine, sine, source, out):
    half = HEAD // 2
    flipped = source.astype(F32).T
    for head in range(out.shape[0] // HEAD):
        low = flipped[head * HEAD : head * HEAD + half]
        high = flipped[head * HEAD + half : (head + 1) * HEAD]
        out[head * HEAD : head * HEAD + half, :] = (low * cosine + high * sine).astype(BF16)
        out[head * HEAD + half : (head + 1) * HEAD, :] = (high * cosine - low * sine).astype(BF16)


def rotate_kernel(own_doc, peer_doc, before_low, before_high, cotangent, peer_cosine, peer_sine, *outs):
    tokens = own_doc.shape[1]
    x = lax.rem(lax.axis_index("fsdp"), 2)

    def start(doc):
        last = jnp.max(doc, axis=1, keepdims=True)
        return tokens - jnp.sum((doc == last).astype(jnp.int32), axis=1, keepdims=True)

    own, peer = start(own_doc[...]), start(peer_doc[...])
    before = start(jnp.where(x == 0, before_low[...], before_high[...]))
    places = lax.broadcasted_iota(jnp.int32, (1, tokens), 1)
    half = HEAD // 2
    steps = lax.broadcasted_iota(jnp.int32, (half, 1), 0).astype(F32)
    frequency = jnp.exp(steps * (-math.log(ROPE_BASE) / half))

    def angles(first, carried):
        offsets = jnp.where(places >= first, places - first, places + tokens - carried)
        return frequency * offsets.astype(F32)

    turned = angles(own, jnp.where(x == 0, before, peer))
    cosine, sine = jnp.cos(turned), jnp.sin(turned)
    width = outs[0].shape[0]
    for part, out in enumerate(outs):
        turn(cosine, sine, cotangent[:, part * width : (part + 1) * width], out)
    turned = angles(peer, jnp.where(x == 0, own, before))
    peer_cosine[...], peer_sine[...] = jnp.cos(turned), jnp.sin(turned)


def peer_kernel(cosine, sine, source, out):
    turn(cosine[...], sine[...], source[:, source.shape[1] - out.shape[0] :], out)


def send_kernel(chunk, place, options, own, peer, features, *refs):
    z, x = spot()
    pieces = dict(zip(options, refs))
    befores, out = refs[len(options) : -1], refs[-1]
    valid = pick(z, [int(d >= 0) for d in chunk])
    where = pick(z, place)
    mine = columns(pick(z, [max(d, 0) for d in chunk]), x, out.shape[1])

    @pl.when(valid == 0)
    def _():
        out[...] = jnp.zeros_like(out)

    for k in options:

        @pl.when((valid == 1) & (where == k))
        def _():
            total = dot(own[...], features[:, mine]) + dot(peer[...], pieces[k][:, : out.shape[1]])
            for before in befores:
                total = total + before[...].astype(F32)
            out[...] = total.astype(BF16)


def own_kernel(own, peer, features, theirs, out):
    z, x = spot()
    out[...] = dot(own[...], features[:, columns(z, x, theirs.shape[1])]) + dot(peer[...], theirs[...])


def inner(scale, cols, total, even, odd, first, second):
    grad = (total[...] + even[...].astype(F32) + odd[...].astype(F32)).T * scale
    fresh_first = 0.9 * first[:, cols] + 0.1 * grad
    fresh_second = 0.95 * second[:, cols] + 0.05 * grad * grad
    return fresh_first, fresh_second


def update_kernel(scale, cols, total, even, odd, first, second, keep, give):
    fresh_first, fresh_second = inner(scale, cols, total, even, odd, first, second)
    count, share, _ = keep.shape
    ours, theirs = halves(fresh_first / (jnp.sqrt(fresh_second) + 1e-08), count, share)
    keep[...] = ours.astype(keep.dtype)
    give[...] = theirs.astype(give.dtype)


def moments_kernel(scale, cols, total, even, odd, first, second, *refs):
    new_first, new_second, done = refs[-3:]
    new_first[...], new_second[...] = inner(scale, cols, total, even, odd, first, second)
    done[...] = jnp.zeros_like(done)


def halves(value, count, share):
    pairs = value.reshape(count, 2, share, value.shape[-1])
    zero = lax.rem(lax.axis_index("rep"), 2) == 0
    return jnp.where(zero, pairs[:, 0], pairs[:, 1]), jnp.where(zero, pairs[:, 1], pairs[:, 0])


def held_kernel(params, came, out):
    count, share, _ = out.shape
    out[...] = halves(params[...], count, share)[0] + halves(came[...], count, share)[0]


def partial_kernel(params, came, mine, other):
    share = mine.shape[0]
    core, near = lax.rem(lax.axis_index("rep"), 2), lax.div(lax.axis_index("rep"), 2)

    def block(at):
        part = pl.ds(pl.multiple_of((2 * at + core) * share, share), share)
        return params[part, :] + came[part, :]

    mine[...] = block(near)
    other[...] = block(1 - near)


def outer_kernel(part, reps, both, came, params_base, far_base, momentum_base, *refs):
    momentum, fresh = refs[-2:]
    near = lax.div(lax.axis_index("rep"), 2) == 0
    mean = (both[...].astype(F32) + came[...].astype(F32)) * (0.2 / reps)
    width = mean.shape[-1]
    cols = slice(part * width, (part + 1) * width)
    mine, far = params_base[:, cols], far_base[:, cols]
    fresh[0] = jnp.where(near, mine, far) - (0.7 * 1.9) * mean[0]
    fresh[1] = jnp.where(near, far, mine) - (0.7 * 1.9) * mean[1]
    momentum[...] = momentum_base[:, cols] + jnp.where(near, mean[0], mean[1])


def assemble_kernel(mine, theirs, *refs):
    out = refs[-1]
    zero = lax.rem(lax.axis_index("rep"), 2) == 0
    a, b = mine[...], theirs[...]
    both = jnp.stack([jnp.where(zero, a, b), jnp.where(zero, b, a)], axis=1)
    out[...] = both.reshape(out.shape)


def here(value):
    return pltpu.with_memory_space_constraint(value, pltpu.HBM)


def after(value, *others):
    return lax.optimization_barrier((value, *others))[0]


def call(kernel, ins, outs, scratch=(), into=None, places=None, cost=1):
    into = into or []
    spaces = list(places or [pltpu.VMEM] * len(ins)) + [pl.ANY] * len(into)
    out_specs, shapes = [], []
    for shape, dtype, *block in outs:
        shapes.append(jax.ShapeDtypeStruct(shape, dtype))
        if block:
            out_specs.append(pl.BlockSpec((shape[0], block[1]), functools.partial(lambda part, i: (0, part), block[0])))
        else:
            out_specs.append(pl.BlockSpec(memory_space=pltpu.VMEM))
    return pl.pallas_call(
        kernel,
        grid=(1,),
        in_specs=[pl.BlockSpec(memory_space=space) for space in spaces],
        out_specs=out_specs,
        out_shape=shapes,
        scratch_shapes=list(scratch),
        input_output_aliases={len(ins) + i: i for i in range(len(into))},
        cost_estimate=pl.CostEstimate(flops=1, transcendentals=0, bytes_accessed=cost),
        compiler_params=pltpu.CompilerParams(vmem_limit_bytes=VMEM_LIMIT),
    )(*ins, *into)


def local(fsdp, reps, activations, key_cotangent, doc_ids, replica_params, first_moment, second_moment, anchor, momentum):
    features, cotangent = activations[0], key_cotangent[0]
    params, first, second = replica_params[0], first_moment[0], second_moment[0]
    tokens, model = features.shape
    keys = cotangent.shape[1]
    rows = model // fsdp
    line = fsdp // 2
    share = anchor.shape[0]
    outer = reps // 2
    width = keys // HALVES
    order, place, sends = schedule(line)

    pair = [(f, f ^ 1) for f in range(fsdp)]
    cores = [(r, r ^ 1) for r in range(reps)]
    across = [(r, r ^ 2) for r in range(reps)]
    evens, odds = [], []
    for z in range(line - 1):
        for x in range(2):
            a, b = 2 * z + x, 2 * z + 2 + x
            (evens if z % 2 == 0 else odds).extend([(a, b), (b, a)])

    first_piece, *raw = call(
        functools.partial(pack_kernel, order, [0]), [here(features), here(cotangent)],
        [((tokens, rows + width), BF16)] + [((tokens, width), BF16)] * (HALVES - 1),
        scratch=[pltpu.SemaphoreType.DMA((1 + HALVES,))], places=[pltpu.HBM] * 2,
    )
    pieces = [lax.ppermute(first_piece, "fsdp", pair)]
    peer_doc = lax.ppermute(doc_ids, "fsdp", pair)
    before_low = lax.ppermute(doc_ids, "fsdp", [(f, f + 1) for f in range(1, fsdp - 1, 2)])
    before_high = lax.ppermute(doc_ids, "fsdp", [(f, f + 2) for f in range(1, fsdp - 2, 2)])

    decay = 1.0 - 0.2 * 0.1
    groups = [[2 * q + c for q in range(outer)] for c in range(2)]
    block = ((outer, share, keys), F32)
    crossed = lax.ppermute(params, "rep", cores)
    if outer == 2:
        mine, ready = call(partial_kernel, [params, crossed], [((share, keys), F32)] * 2)
        summed = mine + lax.ppermute(ready, "rep", across)
    else:
        (held,) = call(held_kernel, [params, crossed], [block])
        summed = lax.psum_scatter(held, "rep", scatter_dimension=0, axis_index_groups=groups, tiled=False)
    base = anchor - (decay / reps) * summed
    momentum_base = 0.9 * momentum + base
    params_base = anchor - 0.7 * (base + 0.9 * momentum_base)
    if outer == 2:
        far_base = lax.ppermute(params_base, "rep", across)
    else:
        bases = lax.all_gather(params_base, "rep", axis_index_groups=groups)

    half = ((HEAD // 2, tokens), F32)
    peer_cosine, peer_sine, *own = call(
        rotate_kernel, [doc_ids, peer_doc, before_low, before_high, after(cotangent, pieces[0], params_base)],
        [half, half] + [((width, tokens), BF16)] * HALVES,
    )
    raw = [pieces[0]] + [lax.ppermute(part, "fsdp", pair) for part in raw]
    peer = [call(peer_kernel, [peer_cosine, peer_sine, part], [((width, tokens), BF16)])[0] for part in raw]
    later = call(
        functools.partial(pack_kernel, order, list(range(1, line))), [here(features)],
        [((tokens, rows), BF16)] * (line - 1),
        scratch=[pltpu.SemaphoreType.DMA((line - 1,))], places=[pltpu.HBM],
    )

    def exchange(k, *done):
        pieces.append(lax.ppermute(after(later[k - 1], *done), "fsdp", pair))

    exchange(1)
    if line > 2:
        exchange(2, peer[0])

    came = [[None, None] for _ in range(HALVES)]
    last = None
    for t, streams in enumerate(sends, 1):
        arrived = [half[::-1] for half in came]
        choices = [sorted({int(place[z][d]) for z, d in enumerate(chunk) if d >= 0}) for chunk in streams]
        turns = [(side, h) for h in range(HALVES) for side in (0, 1) if choices[side]]
        if t == 2:
            turns.sort(key=lambda turn: (turn[1], -turn[0]))
        for side, h in turns:
            chunk, options = streams[side], choices[side]
            spots = [int(place[z][max(d, 0)]) for z, d in enumerate(chunk)]
            waits = [] if last is None else [last]
            if outer == 2 and t == 2:
                waits.append(far_base)
            before = [] if arrived[h][side] is None else [arrived[h][side]]
            (last,) = call(
                functools.partial(send_kernel, chunk, spots, options),
                [after(own[h], *waits), peer[h], features] + [pieces[k] for k in options] + before,
                [((width, rows), BF16)],
            )
            came[h][side] = lax.ppermute(last, "fsdp", odds if side else evens)
            if 2 <= t < line - 1 and (side, h) == (0, 0):
                exchange(t + 1, last)

    scale = 1.0 / math.sqrt(tokens * fsdp)
    new_first = new_second = new_params = new_momentum = None
    momenta, tokens_done = [], []
    for h in range(HALVES):
        cols = slice(h * width, (h + 1) * width)
        mine = after(own[h], last) if h == 0 else own[h]
        (total,) = call(own_kernel, [mine, peer[h], features, pieces[line - 1]], [((width, rows), F32)])
        keep, give = call(
            functools.partial(update_kernel, scale, cols), [total, *came[h], first, second],
            [((outer, share, width), BF16)] * 2,
        )
        both = keep.astype(F32) + lax.ppermute(give, "rep", cores).astype(F32)
        if outer == 2:
            both = both.astype(BF16)
        new_first, new_second, done = call(
            functools.partial(moments_kernel, scale, cols), [after(total, both), *came[h], first, second],
            [((rows, keys), F32, h, width)] * 2 + [((8, 128), F32)], into=[new_first, new_second] if h else None,
            cost=3 * rows * keys * 4,
        )
        tokens_done.append(done)
        if outer == 2:
            ins = [both, lax.ppermute(both, "rep", across), params_base, far_base, momentum_base]
            if h == HALVES - 1:
                ins += tokens_done
            new_momentum, fresh = call(
                functools.partial(outer_kernel, h, reps), ins,
                [((share, keys), F32, h, width), ((outer, share, width), F32)],
                into=[new_momentum] if h else None,
            )
        else:
            part = slice(h * width, (h + 1) * width)
            mean = (0.2 / reps) * lax.psum(both, "rep", axis_index_groups=groups)
            mine = lax.dynamic_index_in_dim(mean, lax.div(lax.axis_index("rep"), 2), 0, keepdims=False)
            momenta.append(momentum_base[:, part] + mine)
            fresh = bases[:, :, part] - (0.7 * 1.9) * mean
        ins = [fresh, lax.ppermute(fresh, "rep", cores)]
        (new_params,) = call(
            assemble_kernel, ins, [((rows, keys), F32, h, width)],
            into=[new_params] if h else None,
        )
    if outer != 2:
        new_momentum = jnp.concatenate(momenta, axis=1)
    return (new_first[None], new_second[None], new_momentum, new_params)


def solution(mesh):
    fsdp, reps = mesh.shape["fsdp"], mesh.shape["rep"]
    placed = (
        P("rep", "fsdp", None),
        P("rep", "fsdp", None),
        P("rep", "fsdp"),
        P("rep", "fsdp", None),
        P("rep", "fsdp", None),
        P("rep", "fsdp", None),
        P(("fsdp", "rep"), None),
        P(("fsdp", "rep"), None),
    )
    return jax.shard_map(
        functools.partial(local, fsdp, reps),
        mesh=mesh,
        in_specs=placed,
        out_specs=(
            P("rep", "fsdp", None),
            P("rep", "fsdp", None),
            P(("fsdp", "rep"), None),
            P("fsdp", None),
        ),
        check_vma=False,
    )
```

```python
import functools
import math

import jax
import jax.numpy as jnp
import numpy as np
from jax import lax
from jax.experimental import pallas as pl
from jax.experimental.pallas import tpu as pltpu
from jax.sharding import PartitionSpec as P

HEAD = 128
ROPE_BASE = 500000.0
HALVES = 2
F32, BF16 = jnp.float32, jnp.bfloat16
VMEM_LIMIT = 16 * 1024 * 1024


def schedule(line):
    order = np.zeros((line, line), np.int32)
    for z in range(line):
        when = {}
        for d in range(line):
            when[d] = line - d + z if d > z else (d + line - z if d < z else 10 * line)
        order[z] = sorted(range(line), key=lambda d: (when[d], abs(d - z) * -1))
    place = np.argsort(order, axis=1)
    sends = []
    for t in range(1, line):
        even, odd = [], []
        for z in range(line):
            right = line - t + z
            right = right if right < line else -1
            left = t - line + z
            left = left if left >= 0 else -1
            even.append(right if z % 2 == 0 else left)
            odd.append(left if z % 2 == 0 else right)
        sends.append((even, odd))
    return order, place, sends


def dot(a, b):
    return lax.dot_general(a, b, (((1,), (0,)), ((), ())), preferred_element_type=F32)


def spot():
    here = lax.axis_index("fsdp")
    return lax.div(here, 2), lax.rem(here, 2)


def pick(index, values):
    total = jnp.int32(0)
    for i, value in enumerate(values):
        if value:
            total = total + jnp.where(index == i, jnp.int32(value), 0)
    return total


def columns(chunk, side, rows):
    return pl.ds(pl.multiple_of((2 * chunk + side) * rows, rows), rows)


def pack_kernel(order, which, features, *refs):
    z, x = spot()
    sems = refs[-1]
    source, outs = (refs[0], refs[1:-1]) if which == [0] else (None, refs[:-1])
    rows = features.shape[1] // (2 * len(order))
    moves = []
    for k, out in zip(which, outs):
        chunk = pick(z, [int(order[p][k]) for p in range(len(order))])
        moves.append((features.at[:, columns(chunk, 1 - x, rows)], out.at[:, :rows]))
    if source is not None:
        width = source.shape[1] // len(outs)
        for at, out in enumerate(outs):
            target = out.at[:, rows:] if at == 0 else out
            moves.append((source.at[:, at * width : (at + 1) * width], target))
    copies = [pltpu.make_async_copy(*move, sems.at[i]) for i, move in enumerate(moves)]
    for copy in copies:
        copy.start()
    for copy in copies:
        copy.wait()


def turn(cosine, sine, source, out):
    half = HEAD // 2
    flipped = source.astype(F32).T
    for head in range(out.shape[0] // HEAD):
        low = flipped[head * HEAD : head * HEAD + half]
        high = flipped[head * HEAD + half : (head + 1) * HEAD]
        out[head * HEAD : head * HEAD + half, :] = (low * cosine + high * sine).astype(BF16)
        out[head * HEAD + half : (head + 1) * HEAD, :] = (high * cosine - low * sine).astype(BF16)


def frequencies():
    half = HEAD // 2
    steps = lax.broadcasted_iota(jnp.int32, (half, 1), 0).astype(F32)
    return jnp.exp(steps * (-math.log(ROPE_BASE) / half))


def table_kernel(doc, cosine, sine):
    angles = frequencies() * lax.broadcasted_iota(jnp.int32, (1, doc.shape[1]), 1).astype(F32)
    cosine[...], sine[...] = jnp.cos(angles), jnp.sin(angles)


def rotate_kernel(own_doc, peer_doc, before_low, before_high, cotangent, cosines, sines, peer_cosine, peer_sine, *outs):
    tokens = own_doc.shape[1]
    x = lax.rem(lax.axis_index("fsdp"), 2)

    def start(doc):
        last = jnp.max(doc, axis=1, keepdims=True)
        return tokens - jnp.sum((doc == last).astype(jnp.int32), axis=1, keepdims=True)

    own, peer = start(own_doc[...]), start(peer_doc[...])
    before = start(jnp.where(x == 0, before_low[...], before_high[...]))
    places = lax.broadcasted_iota(jnp.int32, (1, tokens), 1)
    lanes = lax.broadcasted_iota(jnp.int32, (1, 128), 1)
    own_far = tokens - jnp.where(x == 0, before, peer)
    peer_far = tokens - jnp.where(x == 0, own, before)
    shifts = jnp.where(lanes == 0, -own, jnp.where(lanes == 1, own_far, jnp.where(lanes == 2, -peer, peer_far)))
    turns = frequencies() * shifts.astype(F32)
    shift_cosine, shift_sine = jnp.cos(turns), jnp.sin(turns)

    def table(first, lane):
        late = places >= first
        c = jnp.where(late, shift_cosine[:, lane : lane + 1], shift_cosine[:, lane + 1 : lane + 2])
        s = jnp.where(late, shift_sine[:, lane : lane + 1], shift_sine[:, lane + 1 : lane + 2])
        return cosines[...] * c - sines[...] * s, sines[...] * c + cosines[...] * s

    cosine, sine = table(own, 0)
    width = outs[0].shape[0]
    for part, out in enumerate(outs):
        turn(cosine, sine, cotangent[:, part * width : (part + 1) * width], out)
    peer_cosine[...], peer_sine[...] = table(peer, 2)


def peer_kernel(cosine, sine, source, out):
    turn(cosine[...], sine[...], source[:, source.shape[1] - out.shape[0] :], out)


def send_kernel(chunk, place, options, own, peer, features, *refs):
    z, x = spot()
    pieces = dict(zip(options, refs))
    befores, out = refs[len(options) : -1], refs[-1]
    valid = pick(z, [int(d >= 0) for d in chunk])
    where = pick(z, place)
    mine = columns(pick(z, [max(d, 0) for d in chunk]), x, out.shape[1])

    @pl.when(valid == 0)
    def _():
        out[...] = jnp.zeros_like(out)

    for k in options:

        @pl.when((valid == 1) & (where == k))
        def _():
            total = dot(own[...], features[:, mine]) + dot(peer[...], pieces[k][:, : out.shape[1]])
            for before in befores:
                total = total + before[...].astype(F32)
            out[...] = total.astype(BF16)


def own_kernel(own, peer, features, theirs, out):
    z, x = spot()
    out[...] = dot(own[...], features[:, columns(z, x, theirs.shape[1])]) + dot(peer[...], theirs[...])


def inner(scale, cols, total, even, odd, first, second):
    grad = (total[...] + even[...].astype(F32) + odd[...].astype(F32)).T * scale
    fresh_first = 0.9 * first[:, cols] + 0.1 * grad
    fresh_second = 0.95 * second[:, cols] + 0.05 * grad * grad
    return fresh_first, fresh_second


def update_kernel(scale, cols, total, even, odd, first, second, keep, give):
    fresh_first, fresh_second = inner(scale, cols, total, even, odd, first, second)
    count, share, _ = keep.shape
    ours, theirs = halves(fresh_first / (jnp.sqrt(fresh_second) + 1e-08), count, share)
    keep[...] = ours.astype(keep.dtype)
    give[...] = theirs.astype(give.dtype)


def moments_kernel(scale, cols, total, even, odd, first, second, *refs):
    new_first, new_second, done = refs[-3:]
    new_first[...], new_second[...] = inner(scale, cols, total, even, odd, first, second)
    done[...] = jnp.zeros_like(done)


def halves(value, count, share):
    pairs = value.reshape(count, 2, share, value.shape[-1])
    zero = lax.rem(lax.axis_index("rep"), 2) == 0
    return jnp.where(zero, pairs[:, 0], pairs[:, 1]), jnp.where(zero, pairs[:, 1], pairs[:, 0])


def held_kernel(params, came, out):
    count, share, _ = out.shape
    out[...] = halves(params[...], count, share)[0] + halves(came[...], count, share)[0]


def partial_kernel(params, came, mine, other):
    share = mine.shape[0]
    core, near = lax.rem(lax.axis_index("rep"), 2), lax.div(lax.axis_index("rep"), 2)

    def block(at):
        part = pl.ds(pl.multiple_of((2 * at + core) * share, share), share)
        return params[part, :] + came[part, :]

    mine[...] = block(near)
    other[...] = block(1 - near)


def outer_kernel(part, reps, both, came, params_base, far_base, momentum_base, *refs):
    momentum, fresh = refs[-2:]
    near = lax.div(lax.axis_index("rep"), 2) == 0
    mean = (both[...].astype(F32) + came[...].astype(F32)) * (0.2 / reps)
    width = mean.shape[-1]
    cols = slice(part * width, (part + 1) * width)
    mine, far = params_base[:, cols], far_base[:, cols]
    fresh[0] = jnp.where(near, mine, far) - (0.7 * 1.9) * mean[0]
    fresh[1] = jnp.where(near, far, mine) - (0.7 * 1.9) * mean[1]
    momentum[...] = momentum_base[:, cols] + jnp.where(near, mean[0], mean[1])


def assemble_kernel(mine, theirs, *refs):
    out = refs[-1]
    zero = lax.rem(lax.axis_index("rep"), 2) == 0
    a, b = mine[...], theirs[...]
    both = jnp.stack([jnp.where(zero, a, b), jnp.where(zero, b, a)], axis=1)
    out[...] = both.reshape(out.shape)


def here(value):
    return pltpu.with_memory_space_constraint(value, pltpu.HBM)


def after(value, *others):
    return lax.optimization_barrier((value, *others))[0]


def call(kernel, ins, outs, scratch=(), into=None, places=None, cost=1):
    into = into or []
    spaces = list(places or [pltpu.VMEM] * len(ins)) + [pl.ANY] * len(into)
    out_specs, shapes = [], []
    for shape, dtype, *block in outs:
        shapes.append(jax.ShapeDtypeStruct(shape, dtype))
        if block:
            out_specs.append(pl.BlockSpec((shape[0], block[1]), functools.partial(lambda part, i: (0, part), block[0])))
        else:
            out_specs.append(pl.BlockSpec(memory_space=pltpu.VMEM))
    return pl.pallas_call(
        kernel,
        grid=(1,),
        in_specs=[pl.BlockSpec(memory_space=space) for space in spaces],
        out_specs=out_specs,
        out_shape=shapes,
        scratch_shapes=list(scratch),
        input_output_aliases={len(ins) + i: i for i in range(len(into))},
        cost_estimate=pl.CostEstimate(flops=1, transcendentals=0, bytes_accessed=cost),
        compiler_params=pltpu.CompilerParams(vmem_limit_bytes=VMEM_LIMIT),
    )(*ins, *into)


def local(fsdp, reps, activations, key_cotangent, doc_ids, replica_params, first_moment, second_moment, anchor, momentum):
    features, cotangent = activations[0], key_cotangent[0]
    params, first, second = replica_params[0], first_moment[0], second_moment[0]
    tokens, model = features.shape
    keys = cotangent.shape[1]
    rows = model // fsdp
    line = fsdp // 2
    share = anchor.shape[0]
    outer = reps // 2
    width = keys // HALVES
    order, place, sends = schedule(line)

    pair = [(f, f ^ 1) for f in range(fsdp)]
    cores = [(r, r ^ 1) for r in range(reps)]
    across = [(r, r ^ 2) for r in range(reps)]
    evens, odds = [], []
    for z in range(line - 1):
        for x in range(2):
            a, b = 2 * z + x, 2 * z + 2 + x
            (evens if z % 2 == 0 else odds).extend([(a, b), (b, a)])

    first_piece, *raw = call(
        functools.partial(pack_kernel, order, [0]), [here(features), here(cotangent)],
        [((tokens, rows + width), BF16)] + [((tokens, width), BF16)] * (HALVES - 1),
        scratch=[pltpu.SemaphoreType.DMA((1 + HALVES,))], places=[pltpu.HBM] * 2,
    )
    pieces = [lax.ppermute(first_piece, "fsdp", pair)]
    peer_doc = lax.ppermute(doc_ids, "fsdp", pair)
    before_low = lax.ppermute(doc_ids, "fsdp", [(f, f + 1) for f in range(1, fsdp - 1, 2)])
    before_high = lax.ppermute(doc_ids, "fsdp", [(f, f + 2) for f in range(1, fsdp - 2, 2)])

    decay = 1.0 - 0.2 * 0.1
    groups = [[2 * q + c for q in range(outer)] for c in range(2)]
    block = ((outer, share, keys), F32)
    crossed = lax.ppermute(params, "rep", cores)
    if outer == 2:
        mine, ready = call(partial_kernel, [params, crossed], [((share, keys), F32)] * 2)
        summed = mine + lax.ppermute(ready, "rep", across)
    else:
        (held,) = call(held_kernel, [params, crossed], [block])
        summed = lax.psum_scatter(held, "rep", scatter_dimension=0, axis_index_groups=groups, tiled=False)
    base = anchor - (decay / reps) * summed
    momentum_base = 0.9 * momentum + base
    params_base = anchor - 0.7 * (base + 0.9 * momentum_base)
    if outer == 2:
        far_base = lax.ppermute(params_base, "rep", across)
    else:
        bases = lax.all_gather(params_base, "rep", axis_index_groups=groups)

    half = ((HEAD // 2, tokens), F32)
    cosines, sines = call(table_kernel, [doc_ids], [half] * 2)
    peer_cosine, peer_sine, *own = call(
        rotate_kernel, [doc_ids, peer_doc, before_low, before_high, after(cotangent, pieces[0], params_base), cosines, sines],
        [half, half] + [((width, tokens), BF16)] * HALVES,
    )
    raw = [pieces[0]] + [lax.ppermute(part, "fsdp", pair) for part in raw]
    peer = [call(peer_kernel, [peer_cosine, peer_sine, part], [((width, tokens), BF16)])[0] for part in raw]
    later = call(
        functools.partial(pack_kernel, order, list(range(1, line))), [here(features)],
        [((tokens, rows), BF16)] * (line - 1),
        scratch=[pltpu.SemaphoreType.DMA((line - 1,))], places=[pltpu.HBM],
    )

    def exchange(k, *done):
        pieces.append(lax.ppermute(after(later[k - 1], *done), "fsdp", pair))

    exchange(1)
    if line > 2:
        exchange(2, peer[0])

    came = [[None, None] for _ in range(HALVES)]
    last = None
    for t, streams in enumerate(sends, 1):
        arrived = [half[::-1] for half in came]
        choices = [sorted({int(place[z][d]) for z, d in enumerate(chunk) if d >= 0}) for chunk in streams]
        turns = [(side, h) for h in range(HALVES) for side in (0, 1) if choices[side]]
        if t == 2:
            turns.sort(key=lambda turn: (turn[1], -turn[0]))
        for side, h in turns:
            chunk, options = streams[side], choices[side]
            spots = [int(place[z][max(d, 0)]) for z, d in enumerate(chunk)]
            waits = [] if last is None else [last]
            if outer == 2 and t == 2:
                waits.append(far_base)
            before = [] if arrived[h][side] is None else [arrived[h][side]]
            (last,) = call(
                functools.partial(send_kernel, chunk, spots, options),
                [after(own[h], *waits), peer[h], features] + [pieces[k] for k in options] + before,
                [((width, rows), BF16)],
            )
            came[h][side] = lax.ppermute(last, "fsdp", odds if side else evens)
            if 2 <= t < line - 1 and (side, h) == (0, 0):
                exchange(t + 1, last)

    scale = 1.0 / math.sqrt(tokens * fsdp)
    new_first = new_second = new_params = new_momentum = None
    momenta, tokens_done = [], []
    for h in range(HALVES):
        cols = slice(h * width, (h + 1) * width)
        mine = after(own[h], last) if h == 0 else own[h]
        (total,) = call(own_kernel, [mine, peer[h], features, pieces[line - 1]], [((width, rows), F32)])
        keep, give = call(
            functools.partial(update_kernel, scale, cols), [total, *came[h], first, second],
            [((outer, share, width), BF16)] * 2,
        )
        both = keep.astype(F32) + lax.ppermute(give, "rep", cores).astype(F32)
        if outer == 2:
            both = both.astype(BF16)
        new_first, new_second, done = call(
            functools.partial(moments_kernel, scale, cols), [after(total, both), *came[h], first, second],
            [((rows, keys), F32, h, width)] * 2 + [((8, 128), F32)], into=[new_first, new_second] if h else None,
            cost=3 * rows * keys * 4,
        )
        tokens_done.append(done)
        if outer == 2:
            ins = [both, lax.ppermute(both, "rep", across), params_base, far_base, momentum_base]
            if h == HALVES - 1:
                ins += tokens_done
            new_momentum, fresh = call(
                functools.partial(outer_kernel, h, reps), ins,
                [((share, keys), F32, h, width), ((outer, share, width), F32)],
                into=[new_momentum] if h else None,
            )
        else:
            part = slice(h * width, (h + 1) * width)
            mean = (0.2 / reps) * lax.psum(both, "rep", axis_index_groups=groups)
            mine = lax.dynamic_index_in_dim(mean, lax.div(lax.axis_index("rep"), 2), 0, keepdims=False)
            momenta.append(momentum_base[:, part] + mine)
            fresh = bases[:, :, part] - (0.7 * 1.9) * mean
        ins = [fresh, lax.ppermute(fresh, "rep", cores)]
        (new_params,) = call(
            assemble_kernel, ins, [((rows, keys), F32, h, width)],
            into=[new_params] if h else None,
        )
    if outer != 2:
        new_momentum = jnp.concatenate(momenta, axis=1)
    return (new_first[None], new_second[None], new_momentum, new_params)


def solution(mesh):
    fsdp, reps = mesh.shape["fsdp"], mesh.shape["rep"]
    placed = (
        P("rep", "fsdp", None),
        P("rep", "fsdp", None),
        P("rep", "fsdp"),
        P("rep", "fsdp", None),
        P("rep", "fsdp", None),
        P("rep", "fsdp", None),
        P(("fsdp", "rep"), None),
        P(("fsdp", "rep"), None),
    )
    return jax.shard_map(
        functools.partial(local, fsdp, reps),
        mesh=mesh,
        in_specs=placed,
        out_specs=(
            P("rep", "fsdp", None),
            P("rep", "fsdp", None),
            P(("fsdp", "rep"), None),
            P("fsdp", None),
        ),
        check_vma=False,
    )
```
